32 devices in a mesh: group: 2 (over y), slab: 8 (over z, x), coil: 2 (over core).
Axes of the slice: x: 2, y: 2, z: 4, core: 2. Of those that a mesh axis runs over, the one named last changes fastest.
Arguments:
- image: float32 [2, 8, 256, 192], P(None, ('group', 'coil'), 'slab'), parts along dimension 1, may hold values from -6 to 6
- noise: float32 [2, 8, 256, 192], P(None, ('group', 'coil'), 'slab'), parts along dimension 1, may hold values from -6 to 6
- coil_maps: bfloat16 [2, 32, 8, 256, 192], P(None, 'coil', 'group', 'slab'), parts along dimension 2, may hold values from -2 to 2
- adjoint_data: float32 [2, 8, 256, 192], P(None, ('group', 'coil'), 'slab'), parts along dimension 1, may hold values from -6 to 6
- sampled_lines: int32 [512, 192], P('group'), parts along dimension 0, may hold values 0 or 1
- lift_weight: float32 [2, 128], replicated, may hold values from -4 to 4
- lift_bias: float32 [128], replicated, may hold values from -4 to 4
- conv_one: bfloat16 [27, 128, 128], replicated, may hold values from -0.109375 to 0.109375
- bias_one: float32 [128], replicated, may hold values from -4 to 4
- conv_two: bfloat16 [27, 128, 128], replicated, may hold values from -0.109375 to 0.109375
- bias_two: float32 [128], replicated, may hold values from -4 to 4
- head_weight: float32 [128, 2], replicated, may hold values from -0.5 to 0.5
- head_bias: float32 [2], replicated, may hold values from -4 to 4
Outputs:
- next_image: float32 [2, 8, 256, 192], P(None, ('group', 'coil'), 'slab'), parts along dimension 1
- dc_gradient: float32 [2, 8, 256, 192], P(None, ('group', 'coil'), 'slab'), parts along dimension 1
The draws below stay inside these ranges and needn't reach their ends.
There are 2 independent parts, one for each index of `group`. The reference program is written for one: setup_inputs(seed, part) draws one part's arguments, and reference() takes and returns one part's arrays. A program takes and returns all parts, laid end to end along the dimension named above; an argument that names none is the same for every part. Nothing has to cross between parts.
All inputs are finite; a program needn't handle non-finite values.
Results may differ from the reference program's by a relative error of at most 0.0015.
Values may be sent and summed in bfloat16 or wider, within the bound.
A program may use at most 192 MiB of HBM per device.

```python
import math
import jax
import jax.numpy as jnp
from jax import lax

X = 4
NY = 256
NZ = 192
COILS = 32
C = 128


def touch_ends(entries, own_key, low, largest):
    extent = entries.shape
    index_at = [jax.random.randint(jax.random.fold_in(own_key, axis), (), 0, extent[axis]) for axis in range(len(extent))]
    entries = entries.at[tuple(index_at)].set(low)
    longest = extent.index(max(extent))
    index_at[longest] = (index_at[longest] + 1) % extent[longest]
    return entries.at[tuple(index_at)].set(largest)


def block_scale(own_key, shape, pieces, low, top_value):
    def one(dim, shards_of):
        draws = jax.random.uniform(jax.random.fold_in(jax.random.fold_in(own_key, 6), dim), (shards_of,), jnp.float32, low / len(pieces), top_value / len(pieces))
        return jnp.repeat(jnp.exp(draws), shape[dim] // shards_of).reshape((-1,) + (1,) * (len(shape) - dim - 1))

    loudness = one(*pieces[0])
    for cut in pieces[1:]:
        loudness = loudness * one(*cut)
    return loudness


def normal_values(rng, dims, deviation, bound, pieces=(), kind=jnp.bfloat16):
    gain = block_scale(rng, dims, pieces, -0.22, 0.18) if pieces else 1.0
    values = jax.random.normal(rng, dims, jnp.float32) * deviation * gain
    return jnp.minimum(jnp.maximum(values, -bound), bound).astype(kind)


def setup_inputs(seed: int = 0, part: int = 0) -> dict:
    keys = jax.random.split(jax.random.key(seed), 14)
    part_splits = jax.random.split(jax.random.fold_in(keys[13], part), 14)
    image = normal_values(part_splits[0], (2, X, NY, NZ), 1.0, 6.0, ((1, 2), (2, 8)), jnp.float32)
    noise = normal_values(part_splits[1], (2, X, NY, NZ), 1.0, 6.0, ((1, 2), (2, 8)), jnp.float32)
    coil_maps = normal_values(part_splits[2], (2, COILS, X, NY, NZ), 0.125, 2.0, ((1, 2), (3, 8)))
    adjoint_data = normal_values(part_splits[3], (2, X, NY, NZ), 0.5, 6.0, ((1, 2), (2, 8)), jnp.float32)
    sampled_lines = touch_ends((jax.random.randint(part_splits[4], (NY, NZ), 0, 3) < 1).astype(jnp.int32), jax.random.fold_in(part_splits[4], 1), 0, 1)
    lift_weight = normal_values(keys[5], (2, C), 2 ** -0.5, 4.0, (), jnp.float32)
    lift_bias = normal_values(keys[6], (C,), 0.5, 4.0, (), jnp.float32)
    conv_one = normal_values(keys[7], (27, C, C), (27 * C) ** -0.5, 0.109375)
    bias_one = normal_values(keys[8], (C,), 0.5, 4.0, (), jnp.float32)
    conv_two = normal_values(keys[9], (27, C, C), (27 * C) ** -0.5, 0.109375)
    bias_two = normal_values(keys[10], (C,), 0.5, 4.0, (), jnp.float32)
    head_weight = normal_values(keys[11], (C, 2), C ** -0.5, 0.5, (), jnp.float32)
    head_bias = normal_values(keys[12], (2,), 1.0, 4.0, (), jnp.float32)
    return dict(image=image, noise=noise, coil_maps=coil_maps, adjoint_data=adjoint_data, sampled_lines=sampled_lines, lift_weight=lift_weight, lift_bias=lift_bias, conv_one=conv_one, bias_one=bias_one, conv_two=conv_two, bias_two=bias_two, head_weight=head_weight, head_bias=head_bias)


noise_level = 0.5
step_size = 0.1
data_weight = 2.0

def lift_image(image, lift_weight, lift_bias):
    return jnp.einsum('exyz,ec->xyzc', image, lift_weight, precision=lax.Precision.HIGHEST) + lift_bias

def convolve(features, weight):
    channels = features.shape[-1]
    kernel = weight.astype(jnp.float32).reshape(3, 3, 3, channels, weight.shape[2])
    result = lax.conv_general_dilated(features.astype(jnp.float32)[None], kernel, (1, 1, 1), 'SAME', dimension_numbers=('NDHWC', 'DHWIO', 'NDHWC'), precision=lax.Precision.HIGHEST)
    return result[0]

def reference(image, noise, coil_maps, adjoint_data, sampled_lines, lift_weight, lift_bias, conv_one, bias_one, conv_two, bias_two, head_weight, head_bias):
    lift_sum = lift_image(image, lift_weight, lift_bias)
    act_one = jax.nn.elu(lift_sum).astype(jnp.bfloat16)
    inner = convolve(act_one, conv_one) + bias_one
    act_two = jax.nn.elu(inner).astype(jnp.bfloat16)
    block_sum = lift_sum + convolve(act_two, conv_two) + bias_two
    score = (jnp.einsum('xyzc,ce->exyz', jax.nn.elu(block_sum), head_weight, precision=lax.Precision.HIGHEST) + head_bias[:, None, None, None]) / noise_level
    maps = coil_maps[0].astype(jnp.float32) + 1j * coil_maps[1].astype(jnp.float32)
    field = image[0] + 1j * image[1]
    spectrum = jnp.fft.fft2(maps * field[None], axes=(2, 3), norm='ortho')
    spectrum = spectrum * sampled_lines.astype(jnp.float32)
    returned = jnp.fft.ifft2(spectrum, axes=(2, 3), norm='ortho')
    adjoint = lax.optimization_barrier(jnp.sum(jnp.conj(maps) * returned, axis=0))
    dc_gradient = jnp.stack([jnp.real(adjoint), jnp.imag(adjoint)]) - adjoint_data
    next_image = image + step_size * (score - data_weight * dc_gradient) + math.sqrt(2.0 * step_size) * noise
    return (next_image, dc_gradient)
```

```python
import functools
import math

import jax
import jax.numpy as jnp
import numpy as np
from jax import lax
from jax.experimental import pallas as pl
from jax.experimental.pallas import tpu as pltpu
from jax.sharding import PartitionSpec as P

noise_level = 0.5
step_size = 0.1
data_weight = 2.0
LANES = 128
VMEM_LIMIT = 58 * 1024 * 1024


def elu(value):
    return jnp.where(value > 0, value, jnp.exp(jnp.minimum(value, 0.0)) - 1.0)


def halves(value):
    high = value.astype(jnp.bfloat16)
    low = (value - high.astype(jnp.float32)).astype(jnp.bfloat16)
    return high, low


def split_halves(value):
    high = lax.reduce_precision(value, 8, 7)
    return high.astype(jnp.bfloat16), (value - high).astype(jnp.bfloat16)


def swap_coil(value):
    return lax.ppermute(value, "coil", [(0, 1), (1, 0)])


def store_shifted(scratch, line, value):
    depth, width = value.shape
    position = lax.broadcasted_iota(jnp.int32, value.shape, 0)
    before = jnp.where(position == 0, 0.0, pltpu.roll(value, 1, 0))
    after = jnp.where(position == depth - 1, 0.0, pltpu.roll(value, depth - 1, 0))
    scratch[line, :, 0:width] = before.astype(jnp.bfloat16)
    scratch[line, :, width : 2 * width] = value.astype(jnp.bfloat16)
    scratch[line, :, 2 * width : 3 * width] = after.astype(jnp.bfloat16)


def pack_weights(weight, packed, toward):
    ch = weight.shape[1]
    away = 2 - toward
    zero = jnp.zeros((ch, ch), jnp.bfloat16)
    for tap in range(9):
        mid_w = weight[9 + tap]
        plus_w = weight[9 * toward + tap]
        minus_w = weight[9 * away + tap]
        base = tap * 3 * ch
        packed[base : base + ch, 0:ch] = mid_w
        packed[base : base + ch, ch : 2 * ch] = minus_w
        packed[base + ch : base + 2 * ch, 0:ch] = plus_w
        packed[base + ch : base + 2 * ch, ch : 2 * ch] = mid_w
        packed[base + 2 * ch : base + 3 * ch, 0:ch] = zero
        packed[base + 2 * ch : base + 3 * ch, ch : 2 * ch] = plus_w


def lines_dot(scratch, packed, line, count):
    rows = []
    for j in range(count):
        rows.append(jnp.concatenate([scratch[line + j + dy] for dy in range(3)], axis=1))
    lhs = rows[0] if count == 1 else jnp.concatenate(rows, axis=0)
    return jnp.dot(lhs, packed[...], preferred_element_type=jnp.float32)


def lift_line(lhs, weight):
    return lax.dot_general(
        lhs, weight, (((0,), (0,)), ((), ())), preferred_element_type=jnp.float32
    )


def first_kernel(scalars, lines, lift_w, weight, bias, far, near, scratch, packed, *, block):
    ch = weight.shape[1]
    depth = far.shape[1]
    pack_weights(weight, packed, scalars[0])

    def fill(line, carry):
        store_shifted(scratch, line, elu(lift_line(lines[line], lift_w[...])))
        return carry

    lax.fori_loop(0, lines.shape[0], fill, 0)

    def step(i, carry):
        line = i * block
        act = elu(lines_dot(scratch, packed, line, block) + bias[...])
        for j in range(block):
            keep = jnp.where(scalars[1 + line + j] > 0, 1.0, 0.0)
            part = act[j * depth : (j + 1) * depth] * keep
            far[line + j] = part[:, :ch].astype(jnp.bfloat16)
            near[line + j] = part[:, ch:].astype(jnp.bfloat16)
        return carry

    lax.fori_loop(0, far.shape[0] // block, step, 0)


def second_kernel(
    scalars, far, near, halo, lines, lift_w, weight, bias, head, out, scratch, packed, *, block
):
    ch = weight.shape[1]
    pack_weights(weight, packed, scalars[0])

    def fill(line, carry):
        value = jnp.concatenate([far[line], near[line], halo[line]], axis=1)
        store_shifted(scratch, line, value.astype(jnp.float32))
        return carry

    lax.fori_loop(0, far.shape[0], fill, 0)

    def step(i, carry):
        line = i * block
        total = lines_dot(scratch, packed, line, block) + bias[...]
        lift = [lift_line(lines[line + 2 + j], lift_w[:, : 2 * ch]) for j in range(block)]
        total = total + (lift[0] if block == 1 else jnp.concatenate(lift, axis=0))
        high, low = halves(elu(total))
        contract = (((1,), (1,)), ((), ()))
        out[i] = lax.dot_general(
            head[...], high, contract, preferred_element_type=jnp.float32
        ) + lax.dot_general(head[...], low, contract, preferred_element_type=jnp.float32)
        return carry

    lax.fori_loop(0, out.shape[0], step, 0)


def block_lines(count):
    return 2 if count % 2 == 0 else 1


def params():
    return pltpu.CompilerParams(vmem_limit_bytes=VMEM_LIMIT)


def specs(kinds):
    return [
        pl.BlockSpec(memory_space=pltpu.SMEM if kind == "s" else pltpu.VMEM) for kind in kinds
    ]


def edge_lines(own):
    slab_count = lax.axis_size("slab")
    local_y = own.shape[2]
    first = lax.axis_index("coil") == 0
    near = jnp.where(first, own[:, 1:], own[:, :1])
    flat = ("slab", "coil")

    def moved(block, step, cross):
        pairs = [
            (2 * i + c, 2 * (i + step) + (1 - c if cross else c))
            for i in range(slab_count)
            for c in range(2)
            if 0 <= i + step < slab_count
        ]
        return lax.ppermute(block, flat, pairs)

    last, start = slice(local_y - 2, local_y), slice(0, 2)
    return (
        moved(own[:, :, last], 1, False),
        moved(near[:, :, last], 1, True),
        moved(own[:, :, start], -1, False),
        moved(near[:, :, start], -1, True),
    )


def score_block(
    own,
    partner,
    edges,
    lift_weight,
    lift_bias,
    conv_one,
    bias_one,
    conv_two,
    bias_two,
    head_weight,
):
    ch = lift_weight.shape[1]
    local_y, depth = own.shape[2], own.shape[3]
    coil_pos = lax.axis_index("coil")
    slab_pos = lax.axis_index("slab")
    slab_count = lax.axis_size("slab")
    first = coil_pos == 0
    low_own, low_halo, high_own, high_halo = edges
    partner_near = jnp.where(first, partner[:, :1], partner[:, 1:])
    own = jnp.concatenate([low_own, own, high_own], axis=2)
    halo = jnp.concatenate([low_halo, partner_near, high_halo], axis=2)[:, 0]
    far = jnp.where(first, own[:, 0], own[:, 1])
    near = jnp.where(first, own[:, 1], own[:, 0])
    rows = jnp.stack([far, near, halo])
    total = slab_count * local_y
    line_at = slab_pos * local_y - 2 + jnp.arange(local_y + 4, dtype=jnp.int32)
    valid = jnp.logical_and(line_at >= 0, line_at < total)
    row_hi, row_lo = split_halves(rows)
    ones = jnp.broadcast_to(
        valid.astype(jnp.bfloat16)[None, :, None], (2, local_y + 4, depth)
    )
    stacked = jnp.stack([row_hi, row_hi, row_lo], axis=2)
    stacked = stacked.reshape(18, local_y + 4, depth)
    used = jnp.concatenate([stacked, ones], axis=0)
    used = jnp.pad(used, ((0, 12), (0, 0), (0, 0)))
    lines = jnp.transpose(used, (1, 0, 2))
    w_hi = lax.reduce_precision(lift_weight, 8, 7)
    b_hi = lax.reduce_precision(lift_bias, 8, 7)
    w_rows = jnp.stack([w_hi, lift_weight - w_hi, w_hi], axis=1).reshape(6, ch)
    b_rows = jnp.stack([b_hi, lift_bias - b_hi])
    tall = jnp.concatenate([w_rows] * 3 + [b_rows, jnp.zeros((12, ch), jnp.float32)], axis=0)
    row_at = lax.broadcasted_iota(jnp.int32, (32, 3 * ch), 0)
    col_at = lax.broadcasted_iota(jnp.int32, (32, 3 * ch), 1)
    used_at = jnp.logical_or(row_at // 6 == col_at // ch, row_at >= 18)
    lift_w = jnp.where(used_at, jnp.tile(tall, (1, 3)), 0.0).astype(jnp.bfloat16)
    toward = jnp.where(first, 2, 0).astype(jnp.int32)
    scalars = jnp.concatenate([toward[None], valid[1 : local_y + 3].astype(jnp.int32)])
    block = block_lines(local_y + 2)
    scratches = lambda lines_held: [
        pltpu.VMEM((lines_held, depth, 9 * ch), jnp.bfloat16),
        pltpu.VMEM((27 * ch, 2 * ch), jnp.bfloat16),
    ]
    shape = jax.ShapeDtypeStruct((local_y + 2, depth, ch), jnp.bfloat16)
    far_two, near_two = pl.pallas_call(
        functools.partial(first_kernel, block=block),
        out_shape=(shape, shape),
        in_specs=specs("svvvv"),
        out_specs=tuple(specs("vv")),
        scratch_shapes=scratches(local_y + 4),
        compiler_params=params(),
        name="first_conv",
    )(scalars, lines, lift_w, conv_one, jnp.tile(bias_one, 2)[None])
    halo_two = swap_coil(near_two)
    h_hi, h_lo = split_halves(head_weight.T)
    zero = jnp.zeros_like(h_hi)
    wide = lambda part: jnp.concatenate(
        [jnp.concatenate([part, zero], axis=1), jnp.concatenate([zero, part], axis=1)], axis=0
    )
    head = jnp.concatenate([wide(h_hi), wide(h_lo)], axis=0)
    head = jnp.pad(head, ((0, 8), (0, 0)))
    block = block_lines(local_y)
    scored = pl.pallas_call(
        functools.partial(second_kernel, block=block),
        out_shape=jax.ShapeDtypeStruct((local_y // block, 16, block * depth), jnp.float32),
        in_specs=specs("svvvvvvvv"),
        out_specs=specs("v")[0],
        scratch_shapes=scratches(local_y + 2),
        compiler_params=params(),
        name="second_conv",
    )(
        scalars,
        far_two,
        near_two,
        halo_two,
        lines,
        lift_w,
        conv_two,
        jnp.tile(bias_two, 2)[None],
        head,
    )
    scored = scored[:, 0:4] + scored[:, 4:8]
    scored = scored.reshape(local_y // block, 2, 2, block, depth)
    scored = jnp.transpose(scored, (2, 1, 0, 3, 4)).reshape(2, 2, local_y, depth)
    return jnp.where(first, scored, scored[:, ::-1])


def tables(length):
    index = np.arange(length)
    angle = (index[:, None] * index[None, :] % length) * (2.0 * math.pi / length)

    def parts(values):
        high = values.astype(jnp.bfloat16)
        low = (values - high.astype(np.float64)).astype(jnp.bfloat16)
        return jnp.asarray(np.stack([high, low]))

    return parts(np.cos(angle)), parts(np.sin(angle))


def pair_lanes(first, second):
    depth = first.shape[-1]
    whole = depth // LANES * LANES
    tiles = [p[..., i : i + LANES] for p in (first, second) for i in range(0, whole, LANES)]
    if whole < depth:
        tiles.append(jnp.concatenate([first[..., whole:], second[..., whole:]], axis=-1))
    return jnp.stack(tiles, axis=-3)


def unpair_lanes(tiles, depth):
    count = depth // LANES
    rest = depth - count * LANES
    out = []
    for which in range(2):
        parts = tiles[which * count : (which + 1) * count]
        if rest:
            tail = tiles[2 * count]
            parts = parts + [tail[..., rest * which : rest * which + rest]]
        out.append(parts[0] if len(parts) == 1 else jnp.concatenate(parts, axis=-1))
    return out


def adjoint_kernel(planes, mask, cos_z, sin_z, cos_y, sin_y, out, total_re, total_im, *, coils):
    slabs, _, tiles, local_y, _ = planes.shape
    depth = mask.shape[1]
    whole_y = slabs * local_y

    def pair(k):
        held = [
            planes[:, k, t].reshape(whole_y, LANES).astype(jnp.float32) for t in range(tiles)
        ]
        return unpair_lanes(held, depth)

    def mm(a, b):
        return jnp.dot(a, b, preferred_element_type=jnp.float32)

    def right(a, table):
        return mm(a, table[0]) + mm(a, table[1])

    def left(table, b):
        return mm(table[0], b) + mm(table[1], b)

    total_re[...] = jnp.zeros_like(total_re)
    total_im[...] = jnp.zeros_like(total_im)

    def step(k, carry):
        map_re, map_im = pair(k)
        (u_re, u_im), (low_re, low_im) = pair(coils), pair(coils + 1)
        u_re, u_im = u_re + low_re, u_im + low_im
        c_re = (map_re * u_re - map_im * u_im).astype(jnp.bfloat16)
        c_im = (map_re * u_im + map_im * u_re).astype(jnp.bfloat16)
        f_re = (right(c_re, cos_z) + right(c_im, sin_z)).astype(jnp.bfloat16)
        f_im = (right(c_im, cos_z) - right(c_re, sin_z)).astype(jnp.bfloat16)
        m = mask[...].astype(jnp.float32)
        s_re = ((left(cos_y, f_re) + left(sin_y, f_im)) * m).astype(jnp.bfloat16)
        s_im = ((left(cos_y, f_im) - left(sin_y, f_re)) * m).astype(jnp.bfloat16)
        b_re = (left(cos_y, s_re) - left(sin_y, s_im)).astype(jnp.bfloat16)
        b_im = (left(cos_y, s_im) + left(sin_y, s_re)).astype(jnp.bfloat16)
        r_re = right(b_re, cos_z) - right(b_im, sin_z)
        r_im = right(b_im, cos_z) + right(b_re, sin_z)
        total_re[...] += map_re * r_re + map_im * r_im
        total_im[...] += map_re * r_im - map_im * r_re
        return carry

    lax.fori_loop(0, coils, step, 0)
    shape = (slabs, local_y, LANES)
    count = depth // LANES
    for t in range(count):
        lanes = slice(t * LANES, (t + 1) * LANES)
        out[:, t] = total_re[:, lanes].reshape(shape)
        out[:, count + t] = total_im[:, lanes].reshape(shape)
    if tiles > 2 * count:
        tail = jnp.concatenate([total_re[:, count * LANES :], total_im[:, count * LANES :]], axis=1)
        out[:, 2 * count] = tail.reshape(shape)


def own_share(partial):
    rows = partial.shape[1] // 2
    first = lax.axis_index("coil") == 0
    lower, upper = partial[:, :rows], partial[:, rows:]
    received = swap_coil(jnp.where(first, upper, lower))
    return jnp.where(first, lower, upper) + received


def map_planes(whole, coil_maps):
    slabs = lax.axis_size("slab")
    _, local_coils, readout, local_y, depth = coil_maps.shape
    coil_blocks = slabs // readout
    coils = local_coils // coil_blocks
    maps = pair_lanes(coil_maps[0], coil_maps[1])
    maps = maps.reshape(coil_blocks, coils, readout, *maps.shape[2:])
    maps = jnp.swapaxes(maps, 1, 2).reshape(slabs, coils, *maps.shape[3:])
    u = jnp.stack([pair_lanes(part[0], part[1]) for part in split_halves(whole)], axis=1)
    return jnp.concatenate([maps, jnp.tile(u, (coil_blocks, 1, 1, 1, 1))], axis=1)


def exchanged(value):
    return lax.all_to_all(value, "slab", split_axis=0, concat_axis=0, tiled=True)


def adjoint_by_slice(planes, readout, sampled_lines):
    slabs, count, tiles, local_y, _ = planes.shape
    whole_y, depth = sampled_lines.shape
    combined = pl.pallas_call(
        functools.partial(adjoint_kernel, coils=count - 2),
        out_shape=jax.ShapeDtypeStruct((slabs, tiles, local_y, LANES), jnp.float32),
        in_specs=specs("vvvvvv"),
        out_specs=specs("v")[0],
        scratch_shapes=[pltpu.VMEM((whole_y, depth), jnp.float32)] * 2,
        compiler_params=params(),
        name="adjoint",
    )(planes, sampled_lines, *tables(depth), *tables(whole_y))
    returned = exchanged(combined)
    returned = returned.reshape(slabs // readout, readout, tiles, local_y, LANES)
    partial = jnp.sum(returned, axis=0)
    partial = jnp.stack(unpair_lanes([partial[:, t] for t in range(tiles)], depth))
    return own_share(partial * (1.0 / (whole_y * depth)))


def float_tables(length):
    index = np.arange(length)
    angle = (index[:, None] * index[None, :] % length) * (2.0 * math.pi / length)
    scale = 1.0 / math.sqrt(length)
    return (
        jnp.asarray((np.cos(angle) * scale).astype(np.float32)),
        jnp.asarray((np.sin(angle) * scale).astype(np.float32)),
    )


def adjoint_by_columns(whole, coil_maps, sampled_lines):
    slabs = lax.axis_size("slab")
    slab_pos = lax.axis_index("slab")
    _, local_coils, readout, local_y, depth = coil_maps.shape
    slices = local_coils * readout
    z_blocks = max(1, slabs // math.gcd(slabs, slices))
    width = depth // z_blocks
    maps = coil_maps.astype(jnp.float32)
    map_re, map_im = maps[0], maps[1]
    coil_re = map_re * whole[0][None] - map_im * whole[1][None]
    coil_im = map_re * whole[1][None] + map_im * whole[0][None]
    cos_z, sin_z = (t.reshape(depth, z_blocks, width) for t in float_tables(depth))
    cos_y, sin_y = float_tables(slabs * local_y)
    ein = functools.partial(jnp.einsum, precision=lax.Precision.HIGHEST)
    out = "cxyz,zbk->bcxyk"
    f_re = ein(out, coil_re, cos_z) + ein(out, coil_im, sin_z)
    f_im = ein(out, coil_im, cos_z) - ein(out, coil_re, sin_z)
    each = z_blocks * slices // slabs

    def there(value):
        value = value.reshape(slabs, each, local_y, width).astype(jnp.bfloat16)
        value = lax.all_to_all(value, "slab", split_axis=0, concat_axis=2, tiled=True)
        return value.astype(jnp.float32)

    def back(value):
        value = value.astype(jnp.bfloat16)
        value = lax.all_to_all(value, "slab", split_axis=2, concat_axis=0, tiled=True)
        value = value.astype(jnp.float32)
        return value.reshape(z_blocks, local_coils, readout, local_y, width)

    p_re, p_im = there(f_re), there(f_im)
    block = slab_pos * each // slices
    mask = lax.dynamic_slice_in_dim(sampled_lines.astype(jnp.float32), block * width, width, 1)
    go = "qy,aiyk->aiqk"
    s_re = (ein(go, cos_y, p_re) + ein(go, sin_y, p_im)) * mask
    s_im = (ein(go, cos_y, p_im) - ein(go, sin_y, p_re)) * mask
    home = "qy,aiqk->aiyk"
    b_re = back(ein(home, cos_y, s_re) - ein(home, sin_y, s_im))
    b_im = back(ein(home, cos_y, s_im) + ein(home, sin_y, s_re))
    fin = "bcxyk,zbk->cxyz"
    r_re = ein(fin, b_re, cos_z) - ein(fin, b_im, sin_z)
    r_im = ein(fin, b_im, cos_z) + ein(fin, b_re, sin_z)
    partial = jnp.stack(
        [
            jnp.sum(map_re * r_re + map_im * r_im, axis=0),
            jnp.sum(map_re * r_im - map_im * r_re, axis=0),
        ]
    )
    return own_share(partial)


def local(
    image,
    noise,
    coil_maps,
    adjoint_data,
    sampled_lines,
    lift_weight,
    lift_bias,
    conv_one,
    bias_one,
    conv_two,
    bias_two,
    head_weight,
    head_bias,
):
    slabs = lax.axis_size("slab")
    local_coils, readout = coil_maps.shape[1:3]
    partner = swap_coil(image)
    first = lax.axis_index("coil") == 0
    whole = jnp.where(
        first,
        jnp.concatenate([image, partner], axis=1),
        jnp.concatenate([partner, image], axis=1),
    )
    depth = image.shape[3]
    by_slice = slabs % readout == 0 and local_coils % (slabs // readout) == 0
    by_slice = by_slice and depth % LANES in (0, LANES // 2)
    edges = edge_lines(image)
    if by_slice:
        planes = map_planes(whole, coil_maps)
        planes, edges = lax.optimization_barrier((planes, edges))
        planes = exchanged(planes)
    score = score_block(
        image,
        partner,
        edges,
        lift_weight,
        lift_bias,
        conv_one,
        bias_one,
        conv_two,
        bias_two,
        head_weight,
    )
    score = (score + head_bias[:, None, None, None]) / noise_level
    if by_slice:
        planes, score = lax.optimization_barrier((planes, score))
        adjoint = adjoint_by_slice(planes, readout, sampled_lines)
    else:
        adjoint = adjoint_by_columns(whole, coil_maps, sampled_lines)
    dc_gradient = adjoint - adjoint_data
    next_image = (
        image + step_size * (score - data_weight * dc_gradient) + math.sqrt(2.0 * step_size) * noise
    )
    return (next_image, dc_gradient)


def solution(mesh):
    image_spec = P(None, ("group", "coil"), "slab", None)
    return jax.shard_map(
        local,
        mesh=mesh,
        in_specs=(
            image_spec,
            image_spec,
            P(None, "coil", "group", "slab", None),
            image_spec,
            P("group", None),
        )
        + (P(),) * 8,
        out_specs=(image_spec, image_spec),
        check_vma=False,
    )
```
